512 devices in a mesh: chan: 32 (over y_hi, z), win: 16 (over x, y_lo, core).
Axes of the slice: x: 4, y: 8 (y_hi: 4, y_lo: 2; y = y_hi * 2 + y_lo), z: 8, core: 2. Of those that a mesh axis runs over, the one named last changes fastest.
Arguments:
- traces: float32 [256, 196608], P('chan', 'win')
- offsets: int32 [16], P('win'), may hold values from 0 to 4096
- pair_source: int32 [32, 24], P('chan'), may hold values from 0 to 7
- pair_recv: int32 [32, 24], P('chan'), may hold values from 0 to 7
- pair_hop: int32 [32, 24], P('chan'), may hold values from 0 to 16, never falling along the last dimension, each value on 1 to 2 neighbouring positions
- pair_owner: int32 [768, 1], P('chan'), may hold values from 0 to 31; in each aligned block of 24 rows (0 to 23, 24 to 47, ...) at most 2 rows name the same one
Outputs:
- stacks: float32 [2048, 2, 2048], P('chan', None, 'win')
The draws below stay inside these ranges and needn't reach their ends.
Inputs may be any that keep to these rules, and one draw needn't show every extreme that they name: `pair_hop`: within each block the pairs are ordered by offset index; every offset index has 1 to 2 pairs in a block, and some has exactly 2. `pair_owner`: at most 2 pairs of one block feed one owner, and some owner gets exactly 2.
All inputs are finite; a program needn't handle non-finite values.
Results may differ from the reference program's by a relative error of at most 0.022.
Values may be sent and summed in bfloat16 or wider, within the bound.
A program may use at most 128 MiB of HBM per device.

```python
import math
import jax
import jax.numpy as jnp
import numpy as np
from jax import lax

NT = 8192
F = 2048
SMOOTH_HALF = 32
CH_DEV = 8
SEG_DEV = 1
PAIRS_BLK = 24
HOPS = 8
OFFS = 17
HMOST = 2
CAP = 2
FX = 2112
REC = 12288
CHANNELS = 256
RECORD = 196608
WINDOWS = 16
PAIRS = 768
STACK_ROWS = 2048
N_CHAN = 32
N_WIN = 16


def draw_traces(key, part):
    keys = jax.random.split(key, 3)
    blocking = NT // 8
    pieces = RECORD // blocking
    channel_gain = jnp.exp(jax.random.uniform(keys[1], (CHANNELS, 1, 1), jnp.float32, 0.0, math.log(10.0)))
    block_gain = jnp.exp(jax.random.uniform(keys[2], (CHANNELS, pieces, 1), jnp.float32, 0.0, math.log(10.0)))
    noise = jax.random.normal(keys[0], (CHANNELS, pieces, blocking), jnp.float32)
    return (noise * channel_gain * block_gain).reshape(CHANNELS, RECORD)


def plant(values, own_key, smallest, high):
    dims = values.shape
    spot = [jax.random.randint(jax.random.fold_in(own_key, axis), (), 0, dims[axis]) for axis in range(len(dims))]
    values = values.at[tuple(spot)].set(smallest)
    longest = dims.index(max(dims))
    spot[longest] = (spot[longest] + 1) % dims[longest]
    return values.at[tuple(spot)].set(high)


def length_profile(amount, total, limit, slope):
    portions = [(1 << 20) // math.isqrt(grade ** slope) + 1 for grade in range(2, amount + 1)]
    rest, counts = total - limit - (amount - 1), [1] * (amount - 1)
    while rest > 0:
        movable = [i for i in range(amount - 1) if counts[i] < limit]
        whole, budget = sum([portions[i] for i in movable]), rest
        for i in movable:
            more = min(limit - counts[i], max(1, budget * portions[i] // whole), rest)
            counts[i] = counts[i] + more
            rest = rest - more
    return np.array([limit] + counts)


def ragged_sizes(own_key, number_of, total, bound, slope):
    if number_of == 2:
        one = jax.random.randint(own_key, (), max(1, total - bound), min(bound, total - 1) + 1)
        return jnp.stack([one, total - one])
    tallies = jnp.asarray(length_profile(number_of, total, bound, slope), jnp.int32)
    couples = (number_of - 1) // 2
    donor, taker = tallies[1:1 + 2 * couples:2], tallies[2:2 + 2 * couples:2]
    room = jnp.minimum(donor - 1, bound - taker)
    passed = jax.random.randint(jax.random.fold_in(own_key, 1), (couples,), 0, 1 << 20) % (room + 1)
    tallies = tallies.at[1:1 + 2 * couples:2].set(donor - passed).at[2:2 + 2 * couples:2].set(taker + passed)
    return tallies[jax.random.permutation(jax.random.fold_in(own_key, 2), number_of)]


def routed_block(rng, own, number, rows, number_of, top, limit, lean):
    sequence = jax.random.permutation(rng, number_of)
    heavy_load, usual = shares(number_of, rows * top, limit, lean, True), shares(number_of, rows * top, limit, lean, False)
    places = jnp.arange(number_of)

    def named(tallies, rotation):
        used = int((tallies > 0).sum())
        fixed = max(1, used // 4)
        shifted = fixed + (places - fixed + rotation * (used - fixed)) % max(1, number_of - fixed)
        return jnp.zeros((number_of,), jnp.int32).at[sequence[jnp.where(places < fixed, places, shifted)]].set(jnp.asarray(tallies, jnp.int32))

    tallies = jnp.where(number % 4 == 0, named(heavy_load, number // 4), named(usual, number - number // 4 - 1))
    mixed = jax.random.permutation(jax.random.fold_in(own, 3), number_of)
    giver, receiver = mixed[0:number_of // 2 * 2:2], mixed[1:number_of // 2 * 2:2]
    room = jnp.minimum(tallies[giver] - 1, limit - tallies[receiver]) // 2
    room = jnp.where((giver == sequence[0]) | (receiver == sequence[0]) | (tallies[receiver] == 0), 0, jnp.maximum(room, 0))
    shifted = jax.random.randint(jax.random.fold_in(own, 4), (number_of // 2,), 0, 1 << 20) % (room + 1)
    tallies = tallies.at[giver].add(-shifted).at[receiver].add(shifted)
    labels = jnp.searchsorted(jnp.cumsum(tallies), jnp.arange(rows * top), side="right").astype(jnp.int32)
    table = labels.reshape(top, rows).T
    table = table[jax.random.permutation(jax.random.fold_in(own, 1), rows)]
    rotation = jax.random.randint(jax.random.fold_in(own, 2), (rows, 1), 0, top)
    return jnp.take_along_axis(table, (jnp.arange(top)[None, :] + rotation) % top, axis=1)


def shares(amount, total, bound, lean, full):
    loads = [(1 << 20) // math.isqrt(grade ** lean) + 1 for grade in range(1, amount + 1)]
    largest = bound if full else min(bound, max(-(-total // amount), total * loads[0] // sum(loads)))
    least = 1 if total - largest >= amount - 1 else 0
    given, surplus = [largest] + [least] * (amount - 1), total - largest - least * (amount - 1)
    while surplus > 0:
        candidates = [i for i in range(1, amount) if given[i] < largest] or [i for i in range(1, amount) if given[i] < bound]
        mass, budget = sum([loads[i] for i in candidates]), surplus
        for i in candidates:
            more = min(bound - given[i], max(1, budget * loads[i] // mass), surplus)
            given[i] = given[i] + more
            surplus = surplus - more
    return np.array(given)


def setup_inputs(seed: int = 0) -> dict:
    arg_keys = jax.random.split(jax.random.key(seed), 7)
    traces = draw_traces(jax.random.fold_in(arg_keys[6], 71), 0)
    offsets = plant(jax.random.randint(arg_keys[1], (WINDOWS,), 0, REC - NT + 1), jax.random.fold_in(arg_keys[1], 1), 0, REC - NT).astype(jnp.int32)
    pair_source = plant(jax.random.randint(arg_keys[2], (N_CHAN, PAIRS_BLK), 0, CH_DEV), jax.random.fold_in(arg_keys[2], 1), 0, CH_DEV - 1).astype(jnp.int32)
    pair_recv = plant(jax.random.randint(arg_keys[3], (N_CHAN, PAIRS_BLK), 0, CH_DEV), jax.random.fold_in(arg_keys[3], 1), 0, CH_DEV - 1).astype(jnp.int32)
    pair_hop = jax.vmap(lambda own: jnp.searchsorted(jnp.cumsum(ragged_sizes(own, OFFS, PAIRS_BLK, HMOST, 2)), jnp.arange(PAIRS_BLK), side="right"))(jax.random.split(arg_keys[4], N_CHAN)).reshape((N_CHAN, PAIRS_BLK)).astype(jnp.int32)
    pair_owner_keys = jax.random.split(jax.random.fold_in(arg_keys[5], 1), PAIRS // PAIRS_BLK)
    pair_owner_turns = jax.random.permutation(jax.random.fold_in(arg_keys[5], 3), PAIRS // PAIRS_BLK)
    pair_owner = jax.vmap(lambda own, number: routed_block(jax.random.fold_in(arg_keys[5], 2), own, number, PAIRS_BLK, N_CHAN, 1, CAP, 2))(pair_owner_keys, pair_owner_turns).reshape((PAIRS, 1))
    return dict(traces=traces, offsets=offsets, pair_source=pair_source, pair_recv=pair_recv, pair_hop=pair_hop, pair_owner=pair_owner)


def whiten_rows(segment):
    centred = segment - lax.optimization_barrier(jnp.mean(segment, axis=1, keepdims=True))
    positions = jnp.arange(NT, dtype=jnp.int32).astype(segment.dtype)
    taper = 0.5 - 0.5 * jnp.cos(2.0 * math.pi / NT * positions)
    spectrum = jnp.fft.rfft(centred * taper, axis=1)[:, :FX]
    real_part = jnp.real(spectrum).astype(segment.dtype)
    imag_part = jnp.imag(spectrum).astype(segment.dtype)
    power = real_part * real_part + imag_part * imag_part
    level = lax.reduce_window(power, jnp.zeros((), power.dtype), lax.add, (1, 2 * SMOOTH_HALF + 1), (1, 1), 'VALID') / (2 * SMOOTH_HALF + 1)
    scale = lax.rsqrt(level + 1e-06)
    kept_real = real_part[:, SMOOTH_HALF:SMOOTH_HALF + F] * scale
    kept_imag = imag_part[:, SMOOTH_HALF:SMOOTH_HALF + F] * scale
    return jnp.stack([kept_real, kept_imag], axis=1).astype(jnp.bfloat16)

def reference(traces, offsets, pair_source, pair_recv, pair_hop, pair_owner):

    def one_window(index):
        start = (index // SEG_DEV * REC + offsets[index]).astype(jnp.int32)
        segment = lax.dynamic_slice_in_dim(traces, start, NT, 1)
        return whiten_rows(segment)
    white = lax.map(one_window, jnp.arange(WINDOWS, dtype=jnp.int32))
    owners_all = pair_owner.reshape(N_CHAN, PAIRS_BLK)

    def one_block(block):
        source_ids = block * CH_DEV + pair_source[block]
        target_block = (block + pair_hop[block] - HOPS) % N_CHAN
        receiver_ids = target_block * CH_DEV + pair_recv[block]
        sources = jnp.take(white, source_ids, axis=1).astype(jnp.float32)
        receivers = jnp.take(white, receiver_ids, axis=1).astype(jnp.float32)
        real_part = sources[:, :, 0] * receivers[:, :, 0] + sources[:, :, 1] * receivers[:, :, 1]
        imag_part = sources[:, :, 0] * receivers[:, :, 1] - sources[:, :, 1] * receivers[:, :, 0]
        terms = jnp.stack([real_part, imag_part], axis=2)
        partial_value = lax.optimization_barrier(jnp.sum(terms.reshape(N_WIN, SEG_DEV, PAIRS_BLK, 2, F), axis=1))
        rounded = lax.optimization_barrier(partial_value.astype(jnp.bfloat16)).astype(jnp.float32)
        cross = lax.optimization_barrier(jnp.sum(rounded, axis=0))
        owners = owners_all[block]
        onehot = (owners[:, None] == jnp.arange(N_CHAN, dtype=jnp.int32)[None, :]).astype(jnp.int32)
        earlier = jnp.cumsum(onehot, axis=0) - onehot
        slot = lax.optimization_barrier(jnp.sum(earlier * onehot, axis=1))
        rows = owners * (N_CHAN * CAP) + block * CAP + slot
        return (cross, rows.astype(jnp.int32))
    crosses, rows = lax.map(one_block, jnp.arange(N_CHAN, dtype=jnp.int32))
    stacks = jnp.zeros((STACK_ROWS, 2, F), jnp.float32)
    return stacks.at[rows.reshape(-1)].set(crosses.reshape(-1, 2, F).astype(jnp.float32))
```

```python
import jax
import jax.numpy as jnp
import numpy as np
from jax import lax
from jax.experimental import pallas as pl
from jax.experimental.pallas import tpu as pltpu
from jax.sharding import PartitionSpec as P

MESH = pl.DeviceIdType.MESH
NT = 8192
LANES = 128
ROWS = NT // LANES
BANDS = 16
HALF = 32
CH = 8
NWIN = 16
NCHAN = 32
HOPS = 8
OFFS = 17
PAIRS = 24
REC = 12288
F32 = jnp.float32
BF16 = jnp.bfloat16
HIGH = lax.Precision.HIGHEST


def tables():
    lane = np.arange(LANES)
    row = np.arange(ROWS)
    low = lane + HALF
    angle = 2.0 * np.pi / ROWS * (np.outer(low, row) % ROWS)
    first = np.concatenate([np.cos(angle), -np.sin(angle)], axis=0)
    angle = 2.0 * np.pi / NT * (np.outer(low, lane) % NT)
    twist = np.stack([np.cos(angle), -np.sin(angle)])
    band = np.arange(-1, BANDS + 1)
    angle = 2.0 * np.pi / ROWS * (np.outer(band, lane) % ROWS)
    cos, sin = np.cos(angle), np.sin(angle)
    pad = np.zeros((6, 2 * LANES))
    second = np.concatenate(
        [np.concatenate([cos, sin], axis=1), pad, np.concatenate([-sin, cos], axis=1), pad], axis=0
    )
    place = np.arange(NT).reshape(ROWS, LANES)
    hann = 0.5 - 0.5 * np.cos(2.0 * np.pi / NT * place)
    order = np.zeros((256, 256))
    for ch in range(CH):
        for part in range(2):
            for w in range(NWIN):
                order[ch * 32 + part * 16 + w, w * 16 + part * 8 + ch] = 1.0
    return (
        first.astype(np.float32),
        twist.astype(np.float32),
        second.astype(np.float32),
        hann.astype(np.float32),
        order.astype(jnp.bfloat16),
    )


def kernel(
    offset_ref, source_ref, receiver_ref, hop_ref, owner_ref,
    x_ref, first_ref, twist_ref, second_ref, hann_ref, order_ref,
    out_ref,
    seg_ref, spec_ref, white_ref, all_ref, rows_ref, send_ref, got_ref, cross_ref, mail_ref,
    ask_ref, asked_ref,
    ask_send, ask_recv, win_send, win_recv, hop_send, hop_recv, own_send, own_recv,
):
    mc = lax.axis_index("chan")
    mw = lax.axis_index("win")

    barrier = pltpu.get_barrier_semaphore()

    def greet_win(j, carry):
        pl.semaphore_signal(barrier, inc=1, device_id=(mc, lax.rem(mw + j, NWIN)), device_id_type=MESH)
        return carry

    def greet_chan(j, carry):
        pl.semaphore_signal(barrier, inc=1, device_id=(lax.rem(mc + j, NCHAN), mw), device_id_type=MESH)
        return carry

    lax.fori_loop(1, NWIN, greet_win, 0)
    lax.fori_loop(1, NCHAN, greet_chan, 0)

    def clear(i, carry):
        ask_ref[0, i] = 0
        return carry

    lax.fori_loop(2 * OFFS, LANES, clear, 0)

    def list_offset(h, at):
        nxt = jnp.minimum(at + 1, PAIRS - 1)
        double = jnp.logical_and(at + 1 < PAIRS, hop_ref[0, nxt] == h)
        ask_ref[0, 2 * h] = receiver_ref[0, at]
        ask_ref[0, 2 * h + 1] = receiver_ref[0, nxt]
        return jnp.minimum(at + 1 + double.astype(jnp.int32), PAIRS - 1)

    lax.fori_loop(0, OFFS, list_offset, jnp.int32(0))

    offset = offset_ref[0]
    start = jnp.minimum(offset >> 7, REC // LANES - ROWS - 1)
    shift = offset - start * LANES
    turn = lax.rem(LANES - shift, LANES)
    lane8 = lax.broadcasted_iota(jnp.int32, (CH, LANES), 1)
    keep = lane8 < LANES - shift

    def turned(r):
        return pltpu.roll(x_ref[start + r], turn, 1)

    def shift_row(r, carry):
        before, total = carry
        after = turned(r + 1)
        row = jnp.where(keep, before, after)
        seg_ref[pl.ds(pl.multiple_of(r * CH, CH), CH), :] = row
        return after, total + row

    unused, total = lax.fori_loop(
        0, ROWS, shift_row, (turned(0), jnp.zeros((CH, LANES), F32)), unroll=8
    )
    mean = jnp.sum(total, axis=1, keepdims=True) * (1.0 / NT)
    mean_ref = jnp.broadcast_to(mean, (CH, LANES))

    def centre(r, carry):
        at = pl.ds(pl.multiple_of(r * CH, CH), CH)
        seg_ref[at, :] = seg_ref[at, :] - mean_ref
        return carry

    lax.fori_loop(0, ROWS, centre, 0, unroll=8)

    pl.semaphore_wait(barrier, NWIN - 1 + NCHAN - 1)

    def ask_copy(h):
        return pltpu.make_async_remote_copy(
            src_ref=ask_ref,
            dst_ref=asked_ref.at[pl.ds(h, 1)],
            send_sem=ask_send.at[h],
            recv_sem=ask_recv.at[h],
            device_id=(lax.rem(mc + h + NCHAN - HOPS, NCHAN), mw),
            device_id_type=MESH,
        )

    def far(action):
        def run(j, carry):
            action(j + (j >= HOPS).astype(jnp.int32))
            return carry

        lax.fori_loop(0, OFFS - 1, run, 0)

    far(lambda h: ask_copy(h).start())

    for ch in range(CH):
        data = seg_ref[pl.ds(ch, ROWS, stride=CH), :] * hann_ref[...]
        part = jnp.dot(first_ref[...], data, precision=HIGH, preferred_element_type=F32)
        re, im = part[:LANES], part[LANES:]
        mixed = jnp.concatenate(
            [re * twist_ref[0] - im * twist_ref[1], re * twist_ref[1] + im * twist_ref[0]], axis=1
        )
        bins = lax.dot_general(
            second_ref[...], mixed, (((1,), (1,)), ((), ())), precision=HIGH, preferred_element_type=F32
        )
        spec_ref[0, :, ch, :] = bins[:18]
        spec_ref[1, :, ch, :] = bins[24:42]

    real, imag = spec_ref[0], spec_ref[1]
    power = real * real + imag * imag
    lane = lax.broadcasted_iota(jnp.int32, (1, CH, LANES), 2)

    def ahead(value, by):
        rolled = jnp.stack([pltpu.roll(value[r], LANES - by, 1) for r in range(value.shape[0])])
        later = jnp.concatenate([rolled[1:], rolled[-1:]], axis=0)
        return jnp.where(lane < LANES - by, rolled, later)

    window = power
    for step in (1, 2, 4, 8, 16, 32):
        window = window + ahead(window, step)
    window = window + ahead(power, 64)
    rolled = jnp.stack([pltpu.roll(window[r], HALF, 1) for r in range(BANDS + 1)])
    level = jnp.where(lane >= HALF, rolled[1:], rolled[:-1]) * (1.0 / (2 * HALF + 1))
    scale = lax.rsqrt(level + 1e-06)
    white_ref[...] = jnp.concatenate(
        [real[1 : BANDS + 1] * scale, imag[1 : BANDS + 1] * scale], axis=1
    ).astype(BF16)

    def win_copy(w, slot):
        return pltpu.make_async_remote_copy(
            src_ref=white_ref.at[w],
            dst_ref=all_ref.at[slot],
            send_sem=win_send.at[w],
            recv_sem=win_recv.at[slot],
            device_id=(mc, w),
            device_id_type=MESH,
        )

    def each_win(action):
        def run(j, carry):
            action(lax.rem(mw + j, NWIN))
            return carry

        lax.fori_loop(1, NWIN, run, 0)

    each_win(lambda w: win_copy(w, mw).start())
    all_ref[mw] = white_ref[mw]
    far(lambda h: ask_copy(h).wait_recv())
    each_win(lambda w: win_copy(w, w).wait_recv())

    by_row = jnp.dot(
        order_ref[...], all_ref[...].reshape(NWIN * 16, LANES), preferred_element_type=F32
    )
    rows_ref[...] = by_row.astype(BF16).reshape(CH, 32, LANES)

    def hop_copy(h):
        return pltpu.make_async_remote_copy(
            src_ref=send_ref.at[h],
            dst_ref=got_ref.at[h],
            send_sem=hop_send.at[h],
            recv_sem=hop_recv.at[h],
            device_id=(lax.rem(mc + NCHAN + HOPS - h, NCHAN), mw),
            device_id_type=MESH,
        )

    def hand_out(h):
        send_ref[h, 0] = rows_ref[asked_ref[h, 2 * h]]
        send_ref[h, 1] = rows_ref[asked_ref[h, 2 * h + 1]]
        hop_copy(h).start()

    far(hand_out)
    got_ref[HOPS, 0] = rows_ref[ask_ref[0, 2 * HOPS]]
    got_ref[HOPS, 1] = rows_ref[ask_ref[0, 2 * HOPS + 1]]
    far(lambda h: hop_copy(h).wait_recv())

    for q in range(PAIRS):
        h = hop_ref[0, q]
        place = (hop_ref[0, q - 1] == h).astype(jnp.int32) if q else 0
        mine = rows_ref[source_ref[0, q]].astype(F32)
        theirs = got_ref[h, place].astype(F32)
        mr, mi, tr, ti = mine[:16], mine[16:], theirs[:16], theirs[16:]
        cross_ref[0, pl.ds(q, 1), :] = jnp.sum(mr * tr + mi * ti, axis=0, keepdims=True)
        cross_ref[1, pl.ds(q, 1), :] = jnp.sum(mr * ti - mi * tr, axis=0, keepdims=True)

    column = owner_ref[...]
    up = lax.broadcasted_iota(jnp.int32, (PAIRS, PAIRS), 0)
    along = lax.broadcasted_iota(jnp.int32, (PAIRS, PAIRS), 1)
    names = jnp.sum(jnp.where(up == along, column, 0), axis=0, keepdims=True)
    slot = jnp.sum(
        jnp.where(jnp.logical_and(column == names, up < along), 1, 0), axis=0, keepdims=True
    )
    block = lax.broadcasted_iota(jnp.int32, (NCHAN, PAIRS), 0)
    for s in range(2):
        pick = jnp.where(jnp.logical_and(names == block, slot == s), 1.0, 0.0).astype(F32)
        for part in range(2):
            mail_ref[:, 2 * s + part, :] = jnp.dot(
                pick, cross_ref[part], precision=HIGH, preferred_element_type=F32
            )

    def own_copy(o, from_block):
        return pltpu.make_async_remote_copy(
            src_ref=mail_ref.at[o],
            dst_ref=out_ref.at[from_block],
            send_sem=own_send.at[o],
            recv_sem=own_recv.at[from_block],
            device_id=(o, mw),
            device_id_type=MESH,
        )

    def each_chan(action):
        def run(j, carry):
            action(lax.rem(mc + j, NCHAN))
            return carry

        lax.fori_loop(1, NCHAN, run, 0)

    each_chan(lambda o: own_copy(o, mc).start())
    out_ref[mc] = mail_ref[mc]
    each_chan(lambda o: own_copy(o, o).wait_recv())

    far(lambda h: ask_copy(h).wait_send())
    each_win(lambda w: win_copy(w, mw).wait_send())
    far(lambda h: hop_copy(h).wait_send())
    each_chan(lambda o: own_copy(o, mc).wait_send())


def local(traces, offsets, pair_source, pair_recv, pair_hop, pair_owner):
    pieces = traces.reshape(CH, REC // LANES, LANES).transpose(1, 0, 2)
    consts = [jnp.asarray(t) for t in tables()]
    smem = pl.BlockSpec(memory_space=pltpu.SMEM)
    vmem = pl.BlockSpec(memory_space=pltpu.VMEM)
    out = pl.pallas_call(
        kernel,
        out_shape=jax.ShapeDtypeStruct((NCHAN, 4, LANES), F32),
        in_specs=[smem] * 4 + [vmem] * 7,
        out_specs=vmem,
        scratch_shapes=[
            pltpu.VMEM((ROWS * CH, LANES), F32),
            pltpu.VMEM((2, BANDS + 2, CH, LANES), F32),
            pltpu.VMEM((BANDS, 16, LANES), BF16),
            pltpu.VMEM((NWIN, 16, LANES), BF16),
            pltpu.VMEM((CH, 32, LANES), BF16),
            pltpu.VMEM((OFFS, 2, 32, LANES), BF16),
            pltpu.VMEM((OFFS, 2, 32, LANES), BF16),
            pltpu.VMEM((2, PAIRS, LANES), F32),
            pltpu.VMEM((NCHAN, 4, LANES), F32),
            pltpu.SMEM((1, LANES), jnp.int32),
            pltpu.SMEM((OFFS, LANES), jnp.int32),
            pltpu.SemaphoreType.DMA((OFFS,)),
            pltpu.SemaphoreType.DMA((OFFS,)),
            pltpu.SemaphoreType.DMA((NWIN,)),
            pltpu.SemaphoreType.DMA((NWIN,)),
            pltpu.SemaphoreType.DMA((OFFS,)),
            pltpu.SemaphoreType.DMA((OFFS,)),
            pltpu.SemaphoreType.DMA((NCHAN,)),
            pltpu.SemaphoreType.DMA((NCHAN,)),
        ],
        compiler_params=pltpu.CompilerParams(collective_id=0, has_side_effects=True),
        name="cross_spectra",
    )(offsets, pair_source, pair_recv, pair_hop, pair_owner, pieces, *consts)
    return out.reshape(2 * NCHAN, 2, LANES)


def solution(mesh):
    placed = (
        P("chan", "win"),
        P("win"),
        P("chan", None),
        P("chan", None),
        P("chan", None),
        P("chan", None),
    )
    return jax.shard_map(
        local, mesh=mesh, in_specs=placed, out_specs=P("chan", None, "win"), check_vma=False
    )
```

```python
import jax
import jax.numpy as jnp
import numpy as np
from jax import lax
from jax.experimental import pallas as pl
from jax.experimental.pallas import tpu as pltpu
from jax.sharding import PartitionSpec as P

MESH = pl.DeviceIdType.MESH
NT = 8192
LANES = 128
ROWS = NT // LANES
BANDS = 16
HALF = 32
CH = 8
NWIN = 16
NCHAN = 32
HOPS = 8
OFFS = 17
PAIRS = 24
KEEP = 32
REC = 12288
F32 = jnp.float32
BF16 = jnp.bfloat16
HIGH = lax.Precision.HIGHEST


def split(value):
    high = value.astype(jnp.bfloat16)
    rest = value - high.astype(value.dtype)
    mid = rest.astype(jnp.bfloat16)
    return high, mid, (rest - mid.astype(value.dtype)).astype(jnp.bfloat16)


def tables():
    lane = np.arange(LANES)
    row = np.arange(ROWS)
    low = lane + HALF
    angle = 2.0 * np.pi / ROWS * (np.outer(low[:ROWS], row) % ROWS)
    h, m, w = split(np.concatenate([np.cos(angle), -np.sin(angle)], axis=0))
    first = np.concatenate([h, h, h, m, m, w], axis=1)
    angle = 2.0 * np.pi / NT * (np.outer(low, lane) % NT)
    twist = np.stack([np.cos(angle), -np.sin(angle)])
    band = np.arange(-1, BANDS + 1)
    angle = 2.0 * np.pi / ROWS * (np.outer(band, lane) % ROWS)
    cos, sin = np.cos(angle), np.sin(angle)
    pad = np.zeros((6, 2 * LANES))
    second = np.concatenate(
        [np.concatenate([cos, sin], axis=1), pad, np.concatenate([-sin, cos], axis=1), pad], axis=0
    )
    second = np.concatenate(split(second), axis=0)
    place = np.arange(NT).reshape(ROWS, LANES)
    hann = 0.5 - 0.5 * np.cos(2.0 * np.pi / NT * place)
    order = np.zeros((256, 256))
    for ch in range(CH):
        for part in range(2):
            for w in range(NWIN):
                order[ch * 32 + part * 16 + w, w * 16 + part * 8 + ch] = 1.0
    return (
        first.astype(jnp.bfloat16),
        twist.astype(np.float32),
        second.astype(jnp.bfloat16),
        hann.astype(np.float32),
        order.astype(jnp.bfloat16),
    )


def chan_order():
    steps = [(k, m) for k in range(4) for m in range(8) if k or m]
    return sorted(steps, key=lambda s: -(2 * min(s[0], 4 - s[0]) + min(s[1], 8 - s[1])))


def win_order():
    steps = [(i, j, k) for i in range(4) for j in range(2) for k in range(2) if i or j or k]
    return sorted(steps, key=lambda s: -(min(s[0], 4 - s[0]) + s[1] + 0.1 * s[2]))


HOP_ORDER = tuple(HOPS + d for d in (4, -4, 5, -5, 3, -3, 6, -6, 2, -2, 7, -7, 8, -8, 1, -1))


def kernel(
    offset_hbm, source_hbm, receiver_hbm, hop_hbm, owner_hbm,
    x_hbm, first_hbm, twist_hbm, second_hbm, hann_hbm, order_hbm,
    out_ref,
    offset_ref, source_ref, receiver_ref, hop_ref, owner_ref,
    x_ref, first_ref, twist_ref, second_ref, hann_ref, order_ref,
    seg_ref, spec_ref, white_ref, all_ref, rows_ref, send_ref, got_ref, cross_ref, mail_ref,
    ask_ref, asked_ref,
    in_sem, ask_send, ask_recv, win_send, win_recv, hop_send, hop_recv, own_send, own_recv, own_local,
):
    mc = lax.axis_index("chan")
    mw = lax.axis_index("win")
    chans = [
        lax.rem(mc // 8 + k, 4) * 8 + lax.rem(lax.rem(mc, 8) + m, 8) for k, m in chan_order()
    ]
    wins = [
        lax.rem(mw // 4 + i, 4) * 4 + lax.rem(lax.rem(mw, 4) // 2 + j, 2) * 2 + lax.rem(mw + k, 2)
        for i, j, k in win_order()
    ]

    barrier = pltpu.get_barrier_semaphore()
    for c in chans:
        pl.semaphore_signal(barrier, inc=1, device_id=(c, mw), device_id_type=MESH)
    for w in wins:
        pl.semaphore_signal(barrier, inc=1, device_id=(mc, w), device_id_type=MESH)

    def arrivals(ref, count, send, recv):
        part = ref.at[pl.ds(0, count)]
        return pltpu.make_async_remote_copy(
            src_ref=part, dst_ref=part, send_sem=send, recv_sem=recv, device_id=(mc, mw), device_id_type=MESH
        )

    asks = arrivals(asked_ref, OFFS - 1, ask_send, ask_recv)
    windows = arrivals(all_ref, NWIN - 1, win_send, win_recv)
    hops = arrivals(got_ref, OFFS - 1, hop_send, hop_recv)
    owns = arrivals(mail_ref, NCHAN - 1, own_send, own_recv)

    operands = (
        (offset_hbm, offset_ref), (x_hbm, x_ref), (receiver_hbm, receiver_ref), (hop_hbm, hop_ref),
        (hann_hbm, hann_ref), (first_hbm, first_ref), (twist_hbm, twist_ref), (second_hbm, second_ref),
        (order_hbm, order_ref), (source_hbm, source_ref), (owner_hbm, owner_ref),
    )
    loads = [pltpu.make_async_copy(src, dst, in_sem.at[i]) for i, (src, dst) in enumerate(operands)]
    for load in loads:
        load.start()

    def clear(i, carry):
        ask_ref[0, i] = 0
        return carry

    lax.fori_loop(2 * OFFS, LANES, clear, 0)

    def list_offset(h, at):
        nxt = jnp.minimum(at + 1, PAIRS - 1)
        double = jnp.logical_and(at + 1 < PAIRS, hop_ref[0, nxt] == h)
        ask_ref[0, 2 * h] = receiver_ref[0, at]
        ask_ref[0, 2 * h + 1] = receiver_ref[0, nxt]
        return jnp.minimum(at + 1 + double.astype(jnp.int32), PAIRS - 1)

    loads[2].wait()
    loads[3].wait()
    lax.fori_loop(0, OFFS, list_offset, jnp.int32(0))

    loads[0].wait()
    loads[1].wait()
    offset = offset_ref[0]
    start = jnp.minimum(offset >> 7, REC // LANES - ROWS - 1)
    shift = offset - start * LANES
    turn = lax.rem(LANES - shift, LANES)
    lane8 = lax.broadcasted_iota(jnp.int32, (CH, LANES), 1)
    keep = lane8 < LANES - shift

    def turned(r):
        return pltpu.roll(x_ref[start + r], turn, 1)

    def shift_row(r, carry):
        before, total = carry
        after = turned(r + 1)
        row = jnp.where(keep, before, after)
        seg_ref[pl.ds(pl.multiple_of(r * CH, CH), CH), :] = row
        return after, total + row

    unused, total = lax.fori_loop(
        0, ROWS, shift_row, (turned(0), jnp.zeros((CH, LANES), F32)), unroll=8
    )
    mean = jnp.sum(total, axis=1, keepdims=True) * (1.0 / NT)
    mean_ref = jnp.broadcast_to(mean, (CH, LANES))

    def centre(r, carry):
        at = pl.ds(pl.multiple_of(r * CH, CH), CH)
        seg_ref[at, :] = seg_ref[at, :] - mean_ref
        return carry

    lax.fori_loop(0, ROWS, centre, 0, unroll=8)

    pl.semaphore_wait(barrier, NWIN - 1 + NCHAN - 1)

    def ask_copy(h):
        return pltpu.make_async_remote_copy(
            src_ref=ask_ref,
            dst_ref=asked_ref.at[pl.ds(h, 1)],
            send_sem=ask_send,
            recv_sem=ask_recv,
            device_id=(lax.rem(mc + h + NCHAN - HOPS, NCHAN), mw),
            device_id_type=MESH,
        )

    for h in HOP_ORDER:
        ask_copy(h).start()
    for load in loads[4:]:
        load.wait()

    data = jnp.concatenate(
        [seg_ref[pl.ds(ch, ROWS, stride=CH), :] * hann_ref[...] for ch in range(CH)], axis=1
    )
    high, mid, low = split(data)
    part = jnp.dot(
        first_ref[...],
        jnp.concatenate([high, mid, low, high, mid, high], axis=0),
        preferred_element_type=F32,
    )
    terms = []
    for ch in range(CH):
        at = slice(ch * LANES, (ch + 1) * LANES)
        re = jnp.concatenate([part[:ROWS, at]] * 2, axis=0)
        im = jnp.concatenate([part[ROWS:, at]] * 2, axis=0)
        terms.append(
            split(
                jnp.concatenate(
                    [re * twist_ref[0] - im * twist_ref[1], re * twist_ref[1] + im * twist_ref[0]],
                    axis=1,
                )
            )
        )
    high, mid, low = (jnp.concatenate([t[i] for t in terms], axis=0) for i in range(3))

    def across(rows, value):
        return lax.dot_general(
            second_ref[pl.ds(0, rows), :],
            value,
            (((1,), (1,)), ((), ())),
            preferred_element_type=F32,
        )

    one, two, three = across(144, high), across(96, mid), across(48, low)
    bins = one[:48] + ((one[48:96] + two[:48]) + ((one[96:] + two[48:]) + three))
    for ch in range(CH):
        at = slice(ch * LANES, (ch + 1) * LANES)
        spec_ref[0, :, ch, :] = bins[:18, at]
        spec_ref[1, :, ch, :] = bins[24:42, at]

    real, imag = spec_ref[0], spec_ref[1]
    power = real * real + imag * imag
    lane = lax.broadcasted_iota(jnp.int32, (1, CH, LANES), 2)

    def ahead(value, by):
        rolled = jnp.stack([pltpu.roll(value[r], LANES - by, 1) for r in range(value.shape[0])])
        later = jnp.concatenate([rolled[1:], rolled[-1:]], axis=0)
        return jnp.where(lane < LANES - by, rolled, later)

    window = power
    for step in (1, 2, 4, 8, 16, 32):
        window = window + ahead(window, step)
    window = window + ahead(power, 64)
    rolled = jnp.stack([pltpu.roll(window[r], HALF, 1) for r in range(BANDS + 1)])
    level = jnp.where(lane >= HALF, rolled[1:], rolled[:-1]) * (1.0 / (2 * HALF + 1))
    scale = lax.rsqrt(level + 1e-06)
    white_ref[...] = jnp.concatenate(
        [real[1 : BANDS + 1] * scale, imag[1 : BANDS + 1] * scale], axis=1
    ).astype(BF16)

    def win_copy(w, slot):
        return pltpu.make_async_remote_copy(
            src_ref=white_ref.at[w],
            dst_ref=all_ref.at[slot],
            send_sem=win_send,
            recv_sem=win_recv,
            device_id=(mc, w),
            device_id_type=MESH,
        )

    for w in wins:
        win_copy(w, mw).start()

    all_ref[mw] = white_ref[mw]
    asks.wait_recv()
    windows.wait_recv()

    by_row = jnp.dot(
        order_ref[...], all_ref[...].reshape(NWIN * 16, LANES), preferred_element_type=F32
    )
    rows_ref[...] = by_row.astype(BF16).reshape(CH, 32, LANES)

    def hop_copy(h):
        return pltpu.make_async_remote_copy(
            src_ref=send_ref.at[h],
            dst_ref=got_ref.at[h],
            send_sem=hop_send,
            recv_sem=hop_recv,
            device_id=(lax.rem(mc + NCHAN + HOPS - h, NCHAN), mw),
            device_id_type=MESH,
        )

    def hand_out(h):
        send_ref[h, 0] = rows_ref[asked_ref[h, 2 * h]]
        send_ref[h, 1] = rows_ref[asked_ref[h, 2 * h + 1]]
        hop_copy(h).start()

    for h in HOP_ORDER:
        hand_out(h)

    got_ref[HOPS, 0] = rows_ref[ask_ref[0, 2 * HOPS]]
    got_ref[HOPS, 1] = rows_ref[ask_ref[0, 2 * HOPS + 1]]
    names = owner_ref[...]
    up = lax.broadcasted_iota(jnp.int32, (PAIRS, PAIRS), 0)
    along = lax.broadcasted_iota(jnp.int32, (PAIRS, PAIRS), 1)
    column = jnp.sum(jnp.where(up == along, names, 0), axis=1, keepdims=True)
    slot = jnp.sum(
        jnp.where(jnp.logical_and(column == names, up < along), 1, 0), axis=0, keepdims=True
    )
    block = lax.broadcasted_iota(jnp.int32, (2 * NCHAN, PAIRS), 0)
    place = names + slot * NCHAN
    chosen = jnp.where(place == block, 1.0, 0.0).astype(F32)
    chosen = jnp.concatenate([chosen, jnp.zeros((2 * NCHAN, KEEP - PAIRS), F32)], axis=1)
    pick = jnp.concatenate([chosen] * 3, axis=1).astype(BF16)
    cross_ref[pl.ds(PAIRS, KEEP - PAIRS), :] = jnp.zeros((KEEP - PAIRS, 2 * LANES), F32)

    hops.wait_recv()

    for q in range(PAIRS):
        h = hop_ref[0, q]
        place = (hop_ref[0, q - 1] == h).astype(jnp.int32) if q else 0
        mine = rows_ref[source_ref[0, q]].astype(F32)
        theirs = got_ref[h, place].astype(F32)
        mr, mi, tr, ti = mine[:16], mine[16:], theirs[:16], theirs[16:]
        cross_ref[pl.ds(q, 1), pl.ds(0, LANES)] = jnp.sum(mr * tr + mi * ti, axis=0, keepdims=True)
        cross_ref[pl.ds(q, 1), pl.ds(LANES, LANES)] = jnp.sum(mr * ti - mi * tr, axis=0, keepdims=True)

    high, mid, low = split(cross_ref[...])
    mail = jnp.dot(pick, jnp.concatenate([high, mid, low], axis=0), preferred_element_type=F32)
    for s in range(2):
        for part in range(2):
            mail_ref[:, 2 * s + part, :] = mail[s * NCHAN : (s + 1) * NCHAN, part * LANES : (part + 1) * LANES]

    def own_copy(o, from_block):
        return pltpu.make_async_remote_copy(
            src_ref=mail_ref.at[o],
            dst_ref=out_ref.at[from_block],
            send_sem=own_send,
            recv_sem=own_recv,
            device_id=(o, mw),
            device_id_type=MESH,
        )

    for o in chans:
        own_copy(o, mc).start()

    keep_own = pltpu.make_async_copy(mail_ref.at[mc], out_ref.at[mc], own_local)
    keep_own.start()
    asks.wait_send()
    windows.wait_send()
    hops.wait_send()
    keep_own.wait()
    owns.wait_send()
    owns.wait_recv()


def local(traces, offsets, pair_source, pair_recv, pair_hop, pair_owner):
    pieces = traces.reshape(CH, REC // LANES, LANES).transpose(1, 0, 2)
    consts = [jnp.asarray(t) for t in tables()]
    anywhere = pl.BlockSpec(memory_space=pl.ANY)
    row = (1, PAIRS)
    out = pl.pallas_call(
        kernel,
        out_shape=jax.ShapeDtypeStruct((NCHAN, 4, LANES), F32),
        in_specs=[anywhere] * 11,
        out_specs=anywhere,
        scratch_shapes=[
            pltpu.SMEM((1,), jnp.int32),
            pltpu.SMEM(row, jnp.int32),
            pltpu.SMEM(row, jnp.int32),
            pltpu.SMEM(row, jnp.int32),
            pltpu.VMEM(row, jnp.int32),
            pltpu.VMEM((REC // LANES, CH, LANES), F32),
        ]
        + [pltpu.VMEM(c.shape, c.dtype) for c in consts]
        + [
            pltpu.VMEM((ROWS * CH, LANES), F32),
            pltpu.VMEM((2, BANDS + 2, CH, LANES), F32),
            pltpu.VMEM((BANDS, 16, LANES), BF16),
            pltpu.VMEM((NWIN, 16, LANES), BF16),
            pltpu.VMEM((CH, 32, LANES), BF16),
            pltpu.VMEM((OFFS, 2, 32, LANES), BF16),
            pltpu.VMEM((OFFS, 2, 32, LANES), BF16),
            pltpu.VMEM((KEEP, 2 * LANES), F32),
            pltpu.VMEM((NCHAN, 4, LANES), F32),
            pltpu.SMEM((1, LANES), jnp.int32),
            pltpu.SMEM((OFFS, LANES), jnp.int32),
            pltpu.SemaphoreType.DMA((11,)),
        ]
        + [pltpu.SemaphoreType.DMA] * 9,
        compiler_params=pltpu.CompilerParams(collective_id=0, has_side_effects=True),
        name="cross_spectra",
    )(offsets, pair_source, pair_recv, pair_hop, pair_owner.reshape(row), pieces, *consts)
    return out.reshape(2 * NCHAN, 2, LANES)


def solution(mesh):
    placed = (
        P("chan", "win"),
        P("win"),
        P("chan", None),
        P("chan", None),
        P("chan", None),
        P("chan", None),
    )
    return jax.shard_map(
        local, mesh=mesh, in_specs=placed, out_specs=P("chan", None, "win"), check_vma=False
    )
```

```python
import jax
import jax.numpy as jnp
import numpy as np
from jax import lax
from jax.experimental import pallas as pl
from jax.experimental.pallas import tpu as pltpu
from jax.sharding import PartitionSpec as P

MESH = pl.DeviceIdType.MESH
NT = 8192
LANES = 128
ROWS = NT // LANES
BANDS = 16
HALF = 32
CH = 8
NWIN = 16
NCHAN = 32
HOPS = 8
OFFS = 17
PAIRS = 24
KEEP = 32
REC = 12288
F32 = jnp.float32
BF16 = jnp.bfloat16
HIGH = lax.Precision.HIGHEST


def split(value):
    high = value.astype(jnp.bfloat16)
    rest = value - high.astype(value.dtype)
    mid = rest.astype(jnp.bfloat16)
    return high, mid, (rest - mid.astype(value.dtype)).astype(jnp.bfloat16)


def tables():
    lane = np.arange(LANES)
    row = np.arange(ROWS)
    low = lane + HALF
    angle = 2.0 * np.pi / ROWS * (np.outer(low[:ROWS], row) % ROWS)
    h, m, w = split(np.concatenate([np.cos(angle), -np.sin(angle)], axis=0))
    first = np.concatenate([h, h, h, m, m, w], axis=1)
    angle = 2.0 * np.pi / NT * (np.outer(low, lane) % NT)
    twist = np.stack([np.cos(angle), -np.sin(angle)])
    band = np.arange(-1, BANDS + 1)
    angle = 2.0 * np.pi / ROWS * (np.outer(band, lane) % ROWS)
    cos, sin = np.cos(angle), np.sin(angle)
    pad = np.zeros((6, 2 * LANES))
    second = np.concatenate(
        [np.concatenate([cos, sin], axis=1), pad, np.concatenate([-sin, cos], axis=1), pad], axis=0
    )
    second = np.concatenate(split(second), axis=0)
    place = np.arange(NT).reshape(ROWS, LANES)
    hann = 0.5 - 0.5 * np.cos(2.0 * np.pi / NT * place)
    order = np.zeros((256, 256))
    for ch in range(CH):
        for part in range(2):
            for w in range(NWIN):
                order[ch * 32 + part * 16 + w, w * 16 + part * 8 + ch] = 1.0
    return (
        first.astype(jnp.bfloat16),
        twist.astype(np.float32),
        second.astype(jnp.bfloat16),
        hann.astype(np.float32),
        order.astype(jnp.bfloat16),
    )


def chan_order():
    steps = [(k, m) for k in range(4) for m in range(8) if k or m]
    return sorted(steps, key=lambda s: -(2 * min(s[0], 4 - s[0]) + min(s[1], 8 - s[1])))


def win_order():
    steps = [(i, j, k) for i in range(4) for j in range(2) for k in range(2) if i or j or k]
    return sorted(steps, key=lambda s: -(min(s[0], 4 - s[0]) + s[1] + 0.1 * s[2]))


HOP_ORDER = tuple(HOPS + d for d in (4, -4, 5, -5, 3, -3, 6, -6, 2, -2, 7, -7, 8, -8, 1, -1))


def kernel(
    offset_hbm, source_hbm, receiver_hbm, hop_hbm, owner_hbm,
    x_hbm, first_hbm, twist_hbm, second_hbm, hann_hbm, order_hbm,
    out_ref,
    offset_ref, source_ref, receiver_ref, hop_ref, owner_ref,
    x_ref, first_ref, twist_ref, second_ref, hann_ref, order_ref,
    seg_ref, spec_ref, white_ref, all_ref, rows_ref, send_ref, got_ref, cross_ref, mail_ref,
    ask_ref, asked_ref,
    in_sem, ask_send, ask_recv, win_send, win_recv, hop_send, hop_recv, own_send, own_recv, own_local,
):
    mc = lax.axis_index("chan")
    mw = lax.axis_index("win")
    chans = [
        lax.rem(mc // 8 + k, 4) * 8 + lax.rem(lax.rem(mc, 8) + m, 8) for k, m in chan_order()
    ]
    wins = [
        lax.rem(mw // 4 + i, 4) * 4 + lax.rem(lax.rem(mw, 4) // 2 + j, 2) * 2 + lax.rem(mw + k, 2)
        for i, j, k in win_order()
    ]

    operands = (
        (x_hbm, x_ref), (offset_hbm, offset_ref), (hann_hbm, hann_ref), (first_hbm, first_ref),
        (twist_hbm, twist_ref), (second_hbm, second_ref),
        (receiver_hbm, receiver_ref), (hop_hbm, hop_ref), (order_hbm, order_ref), (source_hbm, source_ref), (owner_hbm, owner_ref),
    )
    loads = [pltpu.make_async_copy(src, dst, in_sem.at[i]) for i, (src, dst) in enumerate(operands)]
    for load in loads[:6]:
        load.start()

    barrier = pltpu.get_barrier_semaphore()
    for c in chans:
        pl.semaphore_signal(barrier, inc=1, device_id=(c, mw), device_id_type=MESH)
    for w in wins:
        pl.semaphore_signal(barrier, inc=1, device_id=(mc, w), device_id_type=MESH)

    for load in loads[6:]:
        load.start()

    def arrivals(ref, count, send, recv):
        part = ref.at[pl.ds(0, count)]
        return pltpu.make_async_remote_copy(
            src_ref=part, dst_ref=part, send_sem=send, recv_sem=recv, device_id=(mc, mw), device_id_type=MESH
        )

    asks = arrivals(asked_ref, OFFS - 1, ask_send, ask_recv)
    windows = arrivals(all_ref, NWIN - 1, win_send, win_recv)
    hops = arrivals(got_ref, OFFS - 1, hop_send, hop_recv)
    owns = arrivals(mail_ref, NCHAN - 1, own_send, own_recv)

    loads[0].wait()
    loads[1].wait()
    offset = offset_ref[0]
    start = jnp.minimum(offset >> 7, REC // LANES - ROWS - 1)
    shift = offset - start * LANES
    turn = lax.rem(LANES - shift, LANES)
    lane8 = lax.broadcasted_iota(jnp.int32, (CH, LANES), 1)
    keep = lane8 < LANES - shift

    def turned(r):
        return pltpu.roll(x_ref[start + r], turn, 1)

    def shift_row(r, carry):
        before, total = carry
        after = turned(r + 1)
        row = jnp.where(keep, before, after)
        seg_ref[pl.ds(pl.multiple_of(r * CH, CH), CH), :] = row
        return after, total + row

    unused, total = lax.fori_loop(
        0, ROWS, shift_row, (turned(0), jnp.zeros((CH, LANES), F32)), unroll=8
    )
    mean = jnp.sum(total, axis=1, keepdims=True) * (1.0 / NT)
    mean_ref = jnp.broadcast_to(mean, (CH, LANES))

    def centre(r, carry):
        at = pl.ds(pl.multiple_of(r * CH, CH), CH)
        seg_ref[at, :] = seg_ref[at, :] - mean_ref
        return carry

    lax.fori_loop(0, ROWS, centre, 0, unroll=8)

    def ask_copy(h):
        return pltpu.make_async_remote_copy(
            src_ref=ask_ref,
            dst_ref=asked_ref.at[pl.ds(h, 1)],
            send_sem=ask_send,
            recv_sem=ask_recv,
            device_id=(lax.rem(mc + h + NCHAN - HOPS, NCHAN), mw),
            device_id_type=MESH,
        )


    for load in loads[2:6]:
        load.wait()
    data = jnp.concatenate(
        [seg_ref[pl.ds(ch, ROWS, stride=CH), :] * hann_ref[...] for ch in range(CH)], axis=1
    )
    high, mid, low = split(data)
    part = jnp.dot(
        first_ref[...],
        jnp.concatenate([high, mid, low, high, mid, high], axis=0),
        preferred_element_type=F32,
    )
    terms = []
    for ch in range(CH):
        at = slice(ch * LANES, (ch + 1) * LANES)
        re = jnp.concatenate([part[:ROWS, at]] * 2, axis=0)
        im = jnp.concatenate([part[ROWS:, at]] * 2, axis=0)
        terms.append(
            split(
                jnp.concatenate(
                    [re * twist_ref[0] - im * twist_ref[1], re * twist_ref[1] + im * twist_ref[0]],
                    axis=1,
                )
            )
        )
    high, mid, low = (jnp.concatenate([t[i] for t in terms], axis=0) for i in range(3))

    def across(rows, value):
        return lax.dot_general(
            second_ref[pl.ds(0, rows), :],
            value,
            (((1,), (1,)), ((), ())),
            preferred_element_type=F32,
        )

    one, two, three = across(144, high), across(96, mid), across(48, low)
    bins = one[:48] + ((one[48:96] + two[:48]) + ((one[96:] + two[48:]) + three))
    for ch in range(CH):
        at = slice(ch * LANES, (ch + 1) * LANES)
        spec_ref[0, :, ch, :] = bins[:18, at]
        spec_ref[1, :, ch, :] = bins[24:42, at]

    real, imag = spec_ref[0], spec_ref[1]
    power = real * real + imag * imag
    lane = lax.broadcasted_iota(jnp.int32, (1, CH, LANES), 2)

    def ahead(value, by):
        rolled = jnp.stack([pltpu.roll(value[r], LANES - by, 1) for r in range(value.shape[0])])
        later = jnp.concatenate([rolled[1:], rolled[-1:]], axis=0)
        return jnp.where(lane < LANES - by, rolled, later)

    window = power
    for step in (1, 2, 4, 8, 16, 32):
        window = window + ahead(window, step)
    window = window + ahead(power, 64)
    rolled = jnp.stack([pltpu.roll(window[r], HALF, 1) for r in range(BANDS + 1)])
    level = jnp.where(lane >= HALF, rolled[1:], rolled[:-1]) * (1.0 / (2 * HALF + 1))
    scale = lax.rsqrt(level + 1e-06)
    white_ref[...] = jnp.concatenate(
        [real[1 : BANDS + 1] * scale, imag[1 : BANDS + 1] * scale], axis=1
    ).astype(BF16)

    def win_copy(w, slot):
        return pltpu.make_async_remote_copy(
            src_ref=white_ref.at[w],
            dst_ref=all_ref.at[slot],
            send_sem=win_send,
            recv_sem=win_recv,
            device_id=(mc, w),
            device_id_type=MESH,
        )

    def clear(i, carry):
        ask_ref[0, i] = 0
        return carry

    lax.fori_loop(2 * OFFS, LANES, clear, 0)

    def list_offset(h, at):
        nxt = jnp.minimum(at + 1, PAIRS - 1)
        double = jnp.logical_and(at + 1 < PAIRS, hop_ref[0, nxt] == h)
        ask_ref[0, 2 * h] = receiver_ref[0, at]
        ask_ref[0, 2 * h + 1] = receiver_ref[0, nxt]
        return jnp.minimum(at + 1 + double.astype(jnp.int32), PAIRS - 1)

    loads[6].wait()
    loads[7].wait()
    lax.fori_loop(0, OFFS, list_offset, jnp.int32(0))

    pl.semaphore_wait(barrier, NWIN - 1 + NCHAN - 1)
    for h in HOP_ORDER:
        ask_copy(h).start()
    for w in wins:
        win_copy(w, mw).start()

    all_ref[mw] = white_ref[mw]
    windows.wait_recv()

    for load in loads[8:]:
        load.wait()
    by_row = jnp.dot(
        order_ref[...], all_ref[...].reshape(NWIN * 16, LANES), preferred_element_type=F32
    )
    rows_ref[...] = by_row.astype(BF16).reshape(CH, 32, LANES)
    asks.wait_recv()

    def hop_copy(h):
        return pltpu.make_async_remote_copy(
            src_ref=send_ref.at[h],
            dst_ref=got_ref.at[h],
            send_sem=hop_send,
            recv_sem=hop_recv,
            device_id=(lax.rem(mc + NCHAN + HOPS - h, NCHAN), mw),
            device_id_type=MESH,
        )

    def hand_out(h):
        send_ref[h, 0] = rows_ref[asked_ref[h, 2 * h]]
        send_ref[h, 1] = rows_ref[asked_ref[h, 2 * h + 1]]
        hop_copy(h).start()

    for h in HOP_ORDER:
        hand_out(h)

    got_ref[HOPS, 0] = rows_ref[ask_ref[0, 2 * HOPS]]
    got_ref[HOPS, 1] = rows_ref[ask_ref[0, 2 * HOPS + 1]]
    names = owner_ref[...]
    up = lax.broadcasted_iota(jnp.int32, (PAIRS, PAIRS), 0)
    along = lax.broadcasted_iota(jnp.int32, (PAIRS, PAIRS), 1)
    column = jnp.sum(jnp.where(up == along, names, 0), axis=1, keepdims=True)
    slot = jnp.sum(
        jnp.where(jnp.logical_and(column == names, up < along), 1, 0), axis=0, keepdims=True
    )
    block = lax.broadcasted_iota(jnp.int32, (2 * NCHAN, PAIRS), 0)
    place = names + slot * NCHAN
    chosen = jnp.where(place == block, 1.0, 0.0).astype(F32)
    chosen = jnp.concatenate([chosen, jnp.zeros((2 * NCHAN, KEEP - PAIRS), F32)], axis=1)
    pick = jnp.concatenate([chosen] * 3, axis=1).astype(BF16)
    cross_ref[pl.ds(PAIRS, KEEP - PAIRS), :] = jnp.zeros((KEEP - PAIRS, 2 * LANES), F32)

    hops.wait_recv()

    for q in range(PAIRS):
        h = hop_ref[0, q]
        place = (hop_ref[0, q - 1] == h).astype(jnp.int32) if q else 0
        mine = rows_ref[source_ref[0, q]].astype(F32)
        theirs = got_ref[h, place].astype(F32)
        mr, mi, tr, ti = mine[:16], mine[16:], theirs[:16], theirs[16:]
        cross_ref[pl.ds(q, 1), pl.ds(0, LANES)] = jnp.sum(mr * tr + mi * ti, axis=0, keepdims=True)
        cross_ref[pl.ds(q, 1), pl.ds(LANES, LANES)] = jnp.sum(mr * ti - mi * tr, axis=0, keepdims=True)

    high, mid, low = split(cross_ref[...])
    mail = jnp.dot(pick, jnp.concatenate([high, mid, low], axis=0), preferred_element_type=F32)
    for s in range(2):
        for part in range(2):
            mail_ref[:, 2 * s + part, :] = mail[s * NCHAN : (s + 1) * NCHAN, part * LANES : (part + 1) * LANES]

    def own_copy(o, from_block):
        return pltpu.make_async_remote_copy(
            src_ref=mail_ref.at[o],
            dst_ref=out_ref.at[from_block],
            send_sem=own_send,
            recv_sem=own_recv,
            device_id=(o, mw),
            device_id_type=MESH,
        )

    for o in chans:
        own_copy(o, mc).start()

    keep_own = pltpu.make_async_copy(mail_ref.at[mc], out_ref.at[mc], own_local)
    keep_own.start()
    asks.wait_send()
    windows.wait_send()
    hops.wait_send()
    keep_own.wait()
    owns.wait_send()
    owns.wait_recv()


def local(traces, offsets, pair_source, pair_recv, pair_hop, pair_owner):
    pieces = traces.reshape(CH, REC // LANES, LANES).transpose(1, 0, 2)
    consts = [jnp.asarray(t) for t in tables()]
    anywhere = pl.BlockSpec(memory_space=pl.ANY)
    row = (1, PAIRS)
    out = pl.pallas_call(
        kernel,
        out_shape=pltpu.VMEM((NCHAN, 4, LANES), F32),
        in_specs=[anywhere] * 11,
        out_specs=anywhere,
        scratch_shapes=[
            pltpu.SMEM((1,), jnp.int32),
            pltpu.SMEM(row, jnp.int32),
            pltpu.SMEM(row, jnp.int32),
            pltpu.SMEM(row, jnp.int32),
            pltpu.VMEM(row, jnp.int32),
            pltpu.VMEM((REC // LANES, CH, LANES), F32),
        ]
        + [pltpu.VMEM(c.shape, c.dtype) for c in consts]
        + [
            pltpu.VMEM((ROWS * CH, LANES), F32),
            pltpu.VMEM((2, BANDS + 2, CH, LANES), F32),
            pltpu.VMEM((BANDS, 16, LANES), BF16),
            pltpu.VMEM((NWIN, 16, LANES), BF16),
            pltpu.VMEM((CH, 32, LANES), BF16),
            pltpu.VMEM((OFFS, 2, 32, LANES), BF16),
            pltpu.VMEM((OFFS, 2, 32, LANES), BF16),
            pltpu.VMEM((KEEP, 2 * LANES), F32),
            pltpu.VMEM((NCHAN, 4, LANES), F32),
            pltpu.SMEM((1, LANES), jnp.int32),
            pltpu.SMEM((OFFS, LANES), jnp.int32),
            pltpu.SemaphoreType.DMA((11,)),
        ]
        + [pltpu.SemaphoreType.DMA] * 9,
        compiler_params=pltpu.CompilerParams(collective_id=0, has_side_effects=True),
        name="cross_spectra",
    )(offsets, pair_source, pair_recv, pair_hop, pair_owner.reshape(row), pieces, *consts)
    return out.reshape(2 * NCHAN, 2, LANES)


def solution(mesh):
    placed = (
        P("chan", "win"),
        P("win"),
        P("chan", None),
        P("chan", None),
        P("chan", None),
        P("chan", None),
    )
    return jax.shard_map(
        local, mesh=mesh, in_specs=placed, out_specs=P("chan", None, "win"), check_vma=False
    )
```

```python
import jax
import jax.numpy as jnp
import numpy as np
from jax import lax
from jax.experimental import pallas as pl
from jax.experimental.pallas import tpu as pltpu
from jax.sharding import PartitionSpec as P

MESH = pl.DeviceIdType.MESH
NT = 8192
LANES = 128
ROWS = NT // LANES
BANDS = 16
HALF = 32
CH = 8
NWIN = 16
NCHAN = 32
HOPS = 8
OFFS = 17
PAIRS = 24
KEEP = 48
GROUPS = 4
SHARE = 4
REC = 12288
F32 = jnp.float32
BF16 = jnp.bfloat16
HIGH = lax.Precision.HIGHEST


def split(value):
    high = value.astype(jnp.bfloat16)
    rest = value - high.astype(value.dtype)
    mid = rest.astype(jnp.bfloat16)
    return high, mid, (rest - mid.astype(value.dtype)).astype(jnp.bfloat16)


def tables():
    lane = np.arange(LANES)
    row = np.arange(ROWS)
    low = lane + HALF
    angle = 2.0 * np.pi / ROWS * (np.outer(low[:ROWS], row) % ROWS)
    h, m, w = split(np.concatenate([np.cos(angle), -np.sin(angle)], axis=0))
    first = np.concatenate([h, h, h, m, m, w], axis=1)
    angle = 2.0 * np.pi / NT * (np.outer(low, lane) % NT)
    twist = np.stack([np.cos(angle), -np.sin(angle)])
    band = np.arange(-1, BANDS + 1)
    angle = 2.0 * np.pi / ROWS * (np.outer(band, lane) % ROWS)
    cos, sin = np.cos(angle), np.sin(angle)
    pad = np.zeros((6, 2 * LANES))
    second = np.concatenate(
        [np.concatenate([cos, sin], axis=1), pad, np.concatenate([-sin, cos], axis=1), pad], axis=0
    )
    second = np.concatenate(split(second), axis=0)
    place = np.arange(NT).reshape(ROWS, LANES)
    hann = 0.5 - 0.5 * np.cos(2.0 * np.pi / NT * place)
    order = np.zeros((256, 256))
    for ch in range(CH):
        for part in range(2):
            for w in range(NWIN):
                order[ch * 32 + part * 16 + w, w * 16 + part * 8 + ch] = 1.0
    return (
        first.astype(jnp.bfloat16),
        twist.astype(np.float32),
        second.astype(jnp.bfloat16),
        hann.astype(np.float32),
        order.astype(jnp.bfloat16),
    )


def chan_order():
    steps = [(k, m) for k in range(4) for m in range(8) if k or m]
    return sorted(steps, key=lambda s: -(2 * min(s[0], 4 - s[0]) + min(s[1], 8 - s[1])))


def win_order():
    steps = [(i, j, k) for i in range(4) for j in range(2) for k in range(2) if i or j or k]
    return sorted(steps, key=lambda s: -(min(s[0], 4 - s[0]) + s[1] + 0.1 * s[2]))


HOP_ORDER = tuple(HOPS + d for d in (4, -4, 5, -5, 3, -3, 6, -6, 2, -2, 7, -7, 8, -8, 1, -1))


def kernel(
    offset_hbm, source_hbm, receiver_hbm, hop_hbm, owner_hbm,
    x_hbm, first_hbm, twist_hbm, second_hbm, hann_hbm, order_hbm,
    out_ref,
    offset_ref, source_ref, receiver_ref, hop_ref, owner_ref, hops_ref,
    x_ref, first_ref, twist_ref, second_ref, hann_ref, order_ref,
    seg_ref, spec_ref, white_ref, all_ref, rows_ref, send_ref, got_ref, cross_ref, mail_ref,
    ask_ref, asked_ref, mine_ref,
    in_sem, ask_send, ask_recv, win_send, win_recv, hop_send, hop_recv, own_send, own_recv, own_local,
):
    mc = lax.axis_index("chan")
    mw = lax.axis_index("win")
    chans = [
        lax.rem(mc // 8 + k, 4) * 8 + lax.rem(lax.rem(mc, 8) + m, 8) for k, m in chan_order()
    ]
    wins = [
        lax.rem(mw // 4 + i, 4) * 4 + lax.rem(lax.rem(mw, 4) // 2 + j, 2) * 2 + lax.rem(mw + k, 2)
        for i, j, k in win_order()
    ]

    operands = (
        (x_hbm, x_ref), (offset_hbm, offset_ref), (hann_hbm, hann_ref), (first_hbm, first_ref),
        (twist_hbm, twist_ref), (second_hbm, second_ref),
        (receiver_hbm, receiver_ref), (hop_hbm, hop_ref), (source_hbm, source_ref), (order_hbm, order_ref), (owner_hbm, owner_ref), (hop_hbm, hops_ref),
    )
    loads = [pltpu.make_async_copy(src, dst, in_sem.at[i]) for i, (src, dst) in enumerate(operands)]
    barrier = pltpu.get_barrier_semaphore()
    for d in HOP_ORDER:
        near = lax.rem(mc + d + NCHAN - HOPS, NCHAN)
        pl.semaphore_signal(barrier, inc=1, device_id=(near, mw), device_id_type=MESH)
    for w in wins:
        pl.semaphore_signal(barrier, inc=1, device_id=(mc, w), device_id_type=MESH)

    for load in loads:
        load.start()

    def arrivals(ref, count, send, recv):
        part = ref.at[pl.ds(0, count)]
        return pltpu.make_async_remote_copy(
            src_ref=part, dst_ref=part, send_sem=send, recv_sem=recv, device_id=(mc, mw), device_id_type=MESH
        )

    asks = arrivals(asked_ref, OFFS - 1, ask_send, ask_recv)
    windows = arrivals(all_ref, NWIN - 1, win_send, win_recv)
    hops = arrivals(got_ref, OFFS - 1, hop_send, hop_recv.at[0])
    owns = arrivals(mail_ref, NCHAN - 1, own_send, own_recv)

    loads[0].wait()
    loads[1].wait()
    offset = offset_ref[0]
    start = jnp.minimum(offset >> 7, REC // LANES - ROWS - 1)
    shift = offset - start * LANES
    turn = lax.rem(LANES - shift, LANES)
    lane8 = lax.broadcasted_iota(jnp.int32, (CH, LANES), 1)
    keep = lane8 < LANES - shift

    def turned(r):
        return pltpu.roll(x_ref[start + r], turn, 1)

    def shift_row(r, carry):
        before, total = carry
        after = turned(r + 1)
        row = jnp.where(keep, before, after)
        seg_ref[pl.ds(pl.multiple_of(r * CH, CH), CH), :] = row
        return after, total + row

    unused, total = lax.fori_loop(
        0, ROWS, shift_row, (turned(0), jnp.zeros((CH, LANES), F32)), unroll=8
    )
    mean = jnp.sum(total, axis=1, keepdims=True) * (1.0 / NT)
    mean_ref = jnp.broadcast_to(mean, (CH, LANES))

    def centre(r, carry):
        at = pl.ds(pl.multiple_of(r * CH, CH), CH)
        seg_ref[at, :] = seg_ref[at, :] - mean_ref
        return carry

    lax.fori_loop(0, ROWS, centre, 0, unroll=8)

    def ask_copy(h):
        return pltpu.make_async_remote_copy(
            src_ref=ask_ref,
            dst_ref=asked_ref.at[pl.ds(h, 1)],
            send_sem=ask_send,
            recv_sem=ask_recv,
            device_id=(lax.rem(mc + h + NCHAN - HOPS, NCHAN), mw),
            device_id_type=MESH,
        )


    for load in loads[2:6]:
        load.wait()
    data = jnp.concatenate(
        [seg_ref[pl.ds(ch, ROWS, stride=CH), :] * hann_ref[...] for ch in range(CH)], axis=1
    )
    high, mid, low = split(data)
    part = jnp.dot(
        first_ref[...],
        jnp.concatenate([high, mid, low, high, mid, high], axis=0),
        preferred_element_type=F32,
    )
    terms = []
    for ch in range(CH):
        at = slice(ch * LANES, (ch + 1) * LANES)
        re = jnp.concatenate([part[:ROWS, at]] * 2, axis=0)
        im = jnp.concatenate([part[ROWS:, at]] * 2, axis=0)
        terms.append(
            split(
                jnp.concatenate(
                    [re * twist_ref[0] - im * twist_ref[1], re * twist_ref[1] + im * twist_ref[0]],
                    axis=1,
                )
            )
        )
    high, mid, low = (jnp.concatenate([t[i] for t in terms], axis=0) for i in range(3))

    def across(rows, value):
        return lax.dot_general(
            second_ref[pl.ds(0, rows), :],
            value,
            (((1,), (1,)), ((), ())),
            preferred_element_type=F32,
        )

    one, two, three = across(144, high), across(96, mid), across(48, low)
    bins = one[:48] + ((one[48:96] + two[:48]) + ((one[96:] + two[48:]) + three))
    for ch in range(CH):
        at = slice(ch * LANES, (ch + 1) * LANES)
        spec_ref[0, :, ch, :] = bins[:18, at]
        spec_ref[1, :, ch, :] = bins[24:42, at]

    real, imag = spec_ref[0], spec_ref[1]
    power = real * real + imag * imag
    lane = lax.broadcasted_iota(jnp.int32, (1, CH, LANES), 2)

    def ahead(value, by):
        rolled = jnp.stack([pltpu.roll(value[r], LANES - by, 1) for r in range(value.shape[0])])
        later = jnp.concatenate([rolled[1:], rolled[-1:]], axis=0)
        return jnp.where(lane < LANES - by, rolled, later)

    window = power
    for step in (1, 2, 4, 8, 16, 32):
        window = window + ahead(window, step)
    window = window + ahead(power, 64)
    rolled = jnp.stack([pltpu.roll(window[r], HALF, 1) for r in range(BANDS + 1)])
    level = jnp.where(lane >= HALF, rolled[1:], rolled[:-1]) * (1.0 / (2 * HALF + 1))
    scale = lax.rsqrt(level + 1e-06)
    white_ref[...] = jnp.concatenate(
        [real[1 : BANDS + 1] * scale, imag[1 : BANDS + 1] * scale], axis=1
    ).astype(BF16)

    def win_copy(w, slot):
        return pltpu.make_async_remote_copy(
            src_ref=white_ref.at[w],
            dst_ref=all_ref.at[slot],
            send_sem=win_send,
            recv_sem=win_recv,
            device_id=(mc, w),
            device_id_type=MESH,
        )

    def clear(i, carry):
        ask_ref[0, i] = 0
        return carry

    lax.fori_loop(2 * OFFS, LANES, clear, 0)

    def list_offset(h, at):
        nxt = jnp.minimum(at + 1, PAIRS - 1)
        double = jnp.logical_and(at + 1 < PAIRS, hop_ref[0, nxt] == h)
        ask_ref[0, 2 * h] = receiver_ref[0, at]
        mine_ref[0, 2 * h] = source_ref[0, at]
        mine_ref[0, 2 * h + 1] = source_ref[0, nxt]
        ask_ref[0, 2 * h + 1] = receiver_ref[0, nxt]
        return jnp.minimum(at + 1 + double.astype(jnp.int32), PAIRS - 1)

    for load in loads[6:9]:
        load.wait()
    lax.fori_loop(0, OFFS, list_offset, jnp.int32(0))

    pl.semaphore_wait(barrier, NWIN - 1 + OFFS - 1)
    for h in HOP_ORDER:
        ask_copy(h).start()
    for w in wins:
        win_copy(w, mw).start()

    all_ref[mw] = white_ref[mw]
    windows.wait_recv()

    for load in loads[9:]:
        load.wait()
    by_row = jnp.dot(
        order_ref[...], all_ref[...].reshape(NWIN * 16, LANES), preferred_element_type=F32
    )
    rows_ref[...] = by_row.astype(BF16).reshape(CH, 32, LANES)
    asks.wait_recv()

    def hop_copy(h):
        return pltpu.make_async_remote_copy(
            src_ref=send_ref.at[h],
            dst_ref=got_ref.at[h],
            send_sem=hop_send,
            recv_sem=hop_recv.at[HOP_ORDER.index(h) // SHARE],
            device_id=(lax.rem(mc + NCHAN + HOPS - h, NCHAN), mw),
            device_id_type=MESH,
        )

    def hand_out(h):
        send_ref[h, 0] = rows_ref[asked_ref[h, 2 * h]]
        send_ref[h, 1] = rows_ref[asked_ref[h, 2 * h + 1]]
        hop_copy(h).start()

    for h in HOP_ORDER:
        hand_out(h)

    got_ref[HOPS, 0] = rows_ref[ask_ref[0, 2 * HOPS]]
    got_ref[HOPS, 1] = rows_ref[ask_ref[0, 2 * HOPS + 1]]
    names = owner_ref[...]
    offs = hops_ref[...]
    up = lax.broadcasted_iota(jnp.int32, (PAIRS, PAIRS), 0)
    along = lax.broadcasted_iota(jnp.int32, (PAIRS, PAIRS), 1)

    def upright(row):
        return jnp.sum(jnp.where(up == along, row, 0), axis=1, keepdims=True)

    def rank(column, row):
        return jnp.sum(
            jnp.where(jnp.logical_and(column == row, along < up), 1, 0), axis=1, keepdims=True
        )

    name, off = upright(names), upright(offs)
    target = name + rank(name, names) * NCHAN + 1
    place = off * 2 + rank(off, offs)
    spot = lax.broadcasted_iota(jnp.int32, (PAIRS, KEEP), 1)
    wanted = jnp.sum(jnp.where(place == spot, target, 0), axis=0, keepdims=True) - 1
    block = lax.broadcasted_iota(jnp.int32, (2 * NCHAN, KEEP), 0)
    chosen = jnp.where(wanted == block, 1.0, 0.0).astype(F32)
    pick = jnp.concatenate([chosen] * 3, axis=1).astype(BF16)
    cross_ref[pl.ds(32, KEEP - 32), :] = jnp.zeros((KEEP - 32, 2 * LANES), F32)

    def cross(h):
        for i in range(2):
            mine = rows_ref[mine_ref[0, 2 * h + i]].astype(F32)
            theirs = got_ref[h, i].astype(F32)
            mr, mi, tr, ti = mine[:16], mine[16:], theirs[:16], theirs[16:]
            at = pl.ds(2 * h + i, 1)
            cross_ref[at, pl.ds(0, LANES)] = jnp.sum(mr * tr + mi * ti, axis=0, keepdims=True)
            cross_ref[at, pl.ds(LANES, LANES)] = jnp.sum(mr * ti - mi * tr, axis=0, keepdims=True)

    cross(HOPS)
    for g in range(GROUPS):
        arrivals(got_ref, SHARE, hop_send, hop_recv.at[g]).wait_recv()
        for h in HOP_ORDER[g * SHARE : (g + 1) * SHARE]:
            cross(h)

    high, mid, low = split(cross_ref[...])
    mail = jnp.dot(pick, jnp.concatenate([high, mid, low], axis=0), preferred_element_type=F32)
    for s in range(2):
        for part in range(2):
            mail_ref[:, 2 * s + part, :] = mail[s * NCHAN : (s + 1) * NCHAN, part * LANES : (part + 1) * LANES]

    def own_copy(o, from_block):
        return pltpu.make_async_remote_copy(
            src_ref=mail_ref.at[o],
            dst_ref=out_ref.at[from_block],
            send_sem=own_send,
            recv_sem=own_recv,
            device_id=(o, mw),
            device_id_type=MESH,
        )

    for o in chans:
        own_copy(o, mc).start()

    keep_own = pltpu.make_async_copy(mail_ref.at[mc], out_ref.at[mc], own_local)
    keep_own.start()
    asks.wait_send()
    windows.wait_send()
    hops.wait_send()
    keep_own.wait()
    owns.wait_send()
    owns.wait_recv()


def local(traces, offsets, pair_source, pair_recv, pair_hop, pair_owner):
    pieces = traces.reshape(CH, REC // LANES, LANES).transpose(1, 0, 2)
    consts = [jnp.asarray(t) for t in tables()]
    anywhere = pl.BlockSpec(memory_space=pl.ANY)
    row = (1, PAIRS)
    out = pl.pallas_call(
        kernel,
        out_shape=pltpu.VMEM((NCHAN, 4, LANES), F32),
        in_specs=[anywhere] * 11,
        out_specs=anywhere,
        scratch_shapes=[
            pltpu.SMEM((1,), jnp.int32),
            pltpu.SMEM(row, jnp.int32),
            pltpu.SMEM(row, jnp.int32),
            pltpu.SMEM(row, jnp.int32),
            pltpu.VMEM(row, jnp.int32),
            pltpu.VMEM(row, jnp.int32),
            pltpu.VMEM((REC // LANES, CH, LANES), F32),
        ]
        + [pltpu.VMEM(c.shape, c.dtype) for c in consts]
        + [
            pltpu.VMEM((ROWS * CH, LANES), F32),
            pltpu.VMEM((2, BANDS + 2, CH, LANES), F32),
            pltpu.VMEM((BANDS, 16, LANES), BF16),
            pltpu.VMEM((NWIN, 16, LANES), BF16),
            pltpu.VMEM((CH, 32, LANES), BF16),
            pltpu.VMEM((OFFS, 2, 32, LANES), BF16),
            pltpu.VMEM((OFFS, 2, 32, LANES), BF16),
            pltpu.VMEM((KEEP, 2 * LANES), F32),
            pltpu.VMEM((NCHAN, 4, LANES), F32),
            pltpu.SMEM((1, LANES), jnp.int32),
            pltpu.SMEM((OFFS, LANES), jnp.int32),
            pltpu.SMEM((1, LANES), jnp.int32),
            pltpu.SemaphoreType.DMA((12,)),
        ]
        + [pltpu.SemaphoreType.DMA] * 5
        + [pltpu.SemaphoreType.DMA((GROUPS,))]
        + [pltpu.SemaphoreType.DMA] * 3,
        compiler_params=pltpu.CompilerParams(collective_id=0, has_side_effects=True),
        name="cross_spectra",
    )(offsets, pair_source, pair_recv, pair_hop, pair_owner.reshape(row), pieces, *consts)
    return out.reshape(2 * NCHAN, 2, LANES)


def solution(mesh):
    placed = (
        P("chan", "win"),
        P("win"),
        P("chan", None),
        P("chan", None),
        P("chan", None),
        P("chan", None),
    )
    return jax.shard_map(
        local, mesh=mesh, in_specs=placed, out_specs=P("chan", None, "win"), check_vma=False
    )
```

```python
import jax
import jax.numpy as jnp
import numpy as np
from jax import lax
from jax.experimental import pallas as pl
from jax.experimental.pallas import tpu as pltpu
from jax.sharding import PartitionSpec as P

MESH = pl.DeviceIdType.MESH
NT = 8192
LANES = 128
ROWS = NT // LANES
BANDS = 16
HALF = 32
CH = 8
NWIN = 16
NCHAN = 32
HOPS = 8
OFFS = 17
PAIRS = 24
KEEP = 48
GROUPS = 8
SHARE = 2
REC = 12288
F32 = jnp.float32
BF16 = jnp.bfloat16
HIGH = lax.Precision.HIGHEST


def split(value):
    high = value.astype(jnp.bfloat16)
    rest = value - high.astype(value.dtype)
    mid = rest.astype(jnp.bfloat16)
    return high, mid, (rest - mid.astype(value.dtype)).astype(jnp.bfloat16)


def tables():
    lane = np.arange(LANES)
    row = np.arange(ROWS)
    low = lane + HALF
    angle = 2.0 * np.pi / ROWS * (np.outer(low[:ROWS], row) % ROWS)
    h, m, w = split(np.concatenate([np.cos(angle), -np.sin(angle)], axis=0))
    first = np.concatenate([h, h, h, m, m, w], axis=1)
    angle = 2.0 * np.pi / NT * (np.outer(low, lane) % NT)
    twist = np.stack([np.cos(angle), -np.sin(angle)])
    band = np.arange(-1, BANDS + 1)
    angle = 2.0 * np.pi / ROWS * (np.outer(band, lane) % ROWS)
    cos, sin = np.cos(angle), np.sin(angle)
    pad = np.zeros((6, 2 * LANES))
    second = np.concatenate(
        [np.concatenate([cos, sin], axis=1), pad, np.concatenate([-sin, cos], axis=1), pad], axis=0
    )
    second = np.concatenate(split(second), axis=0)
    place = np.arange(NT).reshape(ROWS, LANES)
    hann = 0.5 - 0.5 * np.cos(2.0 * np.pi / NT * place)
    order = np.zeros((256, 256))
    for ch in range(CH):
        for part in range(2):
            for w in range(NWIN):
                order[ch * 32 + part * 16 + w, w * 16 + part * 8 + ch] = 1.0
    return (
        first.astype(jnp.bfloat16),
        twist.astype(np.float32),
        second.astype(jnp.bfloat16),
        hann.astype(np.float32),
        order.astype(jnp.bfloat16),
    )


def win_order():
    steps = [(i, j, k) for i in range(4) for j in range(2) for k in range(2) if i or j or k]
    return sorted(steps, key=lambda s: -(min(s[0], 4 - s[0]) + s[1] + 0.1 * s[2]))


HOP_ORDER = tuple(HOPS + d for d in (4, -4, 5, -5, 3, -3, 6, -6, 2, -2, 7, -7, 8, -8, 1, -1))


def kernel(
    offset_hbm, source_hbm, receiver_hbm, hop_hbm, owner_hbm,
    x_hbm, first_hbm, twist_hbm, second_hbm, hann_hbm, order_hbm,
    out_ref,
    offset_ref, source_ref, receiver_ref, hop_ref, owner_ref, hops_ref,
    x_ref, first_ref, twist_ref, second_ref, hann_ref, order_ref,
    seg_ref, spec_ref, white_ref, all_ref, rows_ref, send_ref, got_ref, cross_ref, mail_ref,
    ask_ref, asked_ref, mine_ref,
    in_sem, ask_send, ask_recv, win_send, win_recv, hop_send, hop_recv, own_send, own_recv, own_local,
):
    mc = lax.axis_index("chan")
    mw = lax.axis_index("win")
    wins = [
        lax.rem(mw // 4 + i, 4) * 4 + lax.rem(lax.rem(mw, 4) // 2 + j, 2) * 2 + lax.rem(mw + k, 2)
        for i, j, k in win_order()
    ]

    operands = (
        (x_hbm, x_ref), (offset_hbm, offset_ref), (hann_hbm, hann_ref), (first_hbm, first_ref),
        (twist_hbm, twist_ref), (second_hbm, second_ref),
        (receiver_hbm, receiver_ref), (hop_hbm, hop_ref), (source_hbm, source_ref), (order_hbm, order_ref), (owner_hbm, owner_ref), (hop_hbm, hops_ref),
    )
    loads = [pltpu.make_async_copy(src, dst, in_sem.at[i]) for i, (src, dst) in enumerate(operands)]
    barrier = pltpu.get_barrier_semaphore()
    for d in HOP_ORDER:
        near = lax.rem(mc + d + NCHAN - HOPS, NCHAN)
        pl.semaphore_signal(barrier, inc=1, device_id=(near, mw), device_id_type=MESH)
    for w in wins:
        pl.semaphore_signal(barrier, inc=1, device_id=(mc, w), device_id_type=MESH)

    for load in loads:
        load.start()

    def arrivals(ref, count, send, recv):
        part = ref.at[pl.ds(0, count)]
        return pltpu.make_async_remote_copy(
            src_ref=part, dst_ref=part, send_sem=send, recv_sem=recv, device_id=(mc, mw), device_id_type=MESH
        )

    asks = arrivals(asked_ref, OFFS - 1, ask_send, ask_recv)
    windows = arrivals(all_ref, NWIN - 1, win_send, win_recv)
    hops = arrivals(got_ref, OFFS - 1, hop_send, hop_recv.at[0])
    owns = arrivals(mail_ref, NCHAN - 1, own_send, own_recv)

    loads[0].wait()
    loads[1].wait()
    offset = offset_ref[0]
    start = jnp.minimum(offset >> 7, REC // LANES - ROWS - 1)
    shift = offset - start * LANES
    turn = lax.rem(LANES - shift, LANES)
    lane8 = lax.broadcasted_iota(jnp.int32, (CH, LANES), 1)
    keep = lane8 < LANES - shift

    def turned(r):
        return pltpu.roll(x_ref[start + r], turn, 1)

    def shift_row(r, carry):
        before, total = carry
        after = turned(r + 1)
        row = jnp.where(keep, before, after)
        seg_ref[pl.ds(pl.multiple_of(r * CH, CH), CH), :] = row
        return after, total + row

    unused, total = lax.fori_loop(
        0, ROWS, shift_row, (turned(0), jnp.zeros((CH, LANES), F32)), unroll=8
    )
    mean = jnp.sum(total, axis=1, keepdims=True) * (1.0 / NT)
    mean_ref = jnp.broadcast_to(mean, (CH, LANES))

    def centre(r, carry):
        at = pl.ds(pl.multiple_of(r * CH, CH), CH)
        seg_ref[at, :] = seg_ref[at, :] - mean_ref
        return carry

    lax.fori_loop(0, ROWS, centre, 0, unroll=8)

    def ask_copy(h):
        return pltpu.make_async_remote_copy(
            src_ref=ask_ref,
            dst_ref=asked_ref.at[pl.ds(h, 1)],
            send_sem=ask_send,
            recv_sem=ask_recv,
            device_id=(lax.rem(mc + h + NCHAN - HOPS, NCHAN), mw),
            device_id_type=MESH,
        )


    for load in loads[2:6]:
        load.wait()
    data = jnp.concatenate(
        [seg_ref[pl.ds(ch, ROWS, stride=CH), :] * hann_ref[...] for ch in range(CH)], axis=1
    )
    high, mid, low = split(data)
    part = jnp.dot(
        first_ref[...],
        jnp.concatenate([high, mid, low, high, mid, high], axis=0),
        preferred_element_type=F32,
    )
    terms = []
    for ch in range(CH):
        at = slice(ch * LANES, (ch + 1) * LANES)
        re = jnp.concatenate([part[:ROWS, at]] * 2, axis=0)
        im = jnp.concatenate([part[ROWS:, at]] * 2, axis=0)
        terms.append(
            split(
                jnp.concatenate(
                    [re * twist_ref[0] - im * twist_ref[1], re * twist_ref[1] + im * twist_ref[0]],
                    axis=1,
                )
            )
        )
    high, mid, low = (jnp.concatenate([t[i] for t in terms], axis=0) for i in range(3))

    def across(rows, value):
        return lax.dot_general(
            second_ref[pl.ds(0, rows), :],
            value,
            (((1,), (1,)), ((), ())),
            preferred_element_type=F32,
        )

    one, two, three = across(144, high), across(96, mid), across(48, low)
    bins = one[:48] + ((one[48:96] + two[:48]) + ((one[96:] + two[48:]) + three))
    for ch in range(CH):
        at = slice(ch * LANES, (ch + 1) * LANES)
        spec_ref[0, :, ch, :] = bins[:18, at]
        spec_ref[1, :, ch, :] = bins[24:42, at]

    real, imag = spec_ref[0], spec_ref[1]
    power = real * real + imag * imag
    lane = lax.broadcasted_iota(jnp.int32, (1, CH, LANES), 2)

    def ahead(value, by):
        rolled = jnp.stack([pltpu.roll(value[r], LANES - by, 1) for r in range(value.shape[0])])
        later = jnp.concatenate([rolled[1:], rolled[-1:]], axis=0)
        return jnp.where(lane < LANES - by, rolled, later)

    window = power
    for step in (1, 2, 4, 8, 16, 32):
        window = window + ahead(window, step)
    window = window + ahead(power, 64)
    rolled = jnp.stack([pltpu.roll(window[r], HALF, 1) for r in range(BANDS + 1)])
    level = jnp.where(lane >= HALF, rolled[1:], rolled[:-1]) * (1.0 / (2 * HALF + 1))
    scale = lax.rsqrt(level + 1e-06)
    white_ref[...] = jnp.concatenate(
        [real[1 : BANDS + 1] * scale, imag[1 : BANDS + 1] * scale], axis=1
    ).astype(BF16)

    def win_copy(w, slot):
        return pltpu.make_async_remote_copy(
            src_ref=white_ref.at[w],
            dst_ref=all_ref.at[slot],
            send_sem=win_send,
            recv_sem=win_recv,
            device_id=(mc, w),
            device_id_type=MESH,
        )

    def clear(i, carry):
        ask_ref[0, i] = 0
        return carry

    lax.fori_loop(2 * OFFS, LANES, clear, 0)

    def list_offset(h, at):
        nxt = jnp.minimum(at + 1, PAIRS - 1)
        double = jnp.logical_and(at + 1 < PAIRS, hop_ref[0, nxt] == h)
        ask_ref[0, 2 * h] = receiver_ref[0, at]
        mine_ref[0, 2 * h] = source_ref[0, at]
        mine_ref[0, 2 * h + 1] = source_ref[0, nxt]
        ask_ref[0, 2 * h + 1] = receiver_ref[0, nxt]
        return jnp.minimum(at + 1 + double.astype(jnp.int32), PAIRS - 1)

    for load in loads[6:9]:
        load.wait()
    lax.fori_loop(0, OFFS, list_offset, jnp.int32(0))

    pl.semaphore_wait(barrier, NWIN - 1 + OFFS - 1)
    for h in HOP_ORDER:
        ask_copy(h).start()
    for w in wins:
        win_copy(w, mw).start()

    all_ref[mw] = white_ref[mw]
    windows.wait_recv()

    for load in loads[9:]:
        load.wait()
    by_row = jnp.dot(
        order_ref[...], all_ref[...].reshape(NWIN * 16, LANES), preferred_element_type=F32
    )
    rows_ref[...] = by_row.astype(BF16).reshape(CH, 32, LANES)
    asks.wait_recv()

    def hop_copy(h):
        return pltpu.make_async_remote_copy(
            src_ref=send_ref.at[h],
            dst_ref=got_ref.at[h],
            send_sem=hop_send,
            recv_sem=hop_recv.at[HOP_ORDER.index(h) // SHARE],
            device_id=(lax.rem(mc + NCHAN + HOPS - h, NCHAN), mw),
            device_id_type=MESH,
        )

    def hand_out(h):
        send_ref[h, 0] = rows_ref[asked_ref[h, 2 * h]]
        send_ref[h, 1] = rows_ref[asked_ref[h, 2 * h + 1]]
        hop_copy(h).start()

    for h in HOP_ORDER:
        hand_out(h)

    got_ref[HOPS, 0] = rows_ref[ask_ref[0, 2 * HOPS]]
    got_ref[HOPS, 1] = rows_ref[ask_ref[0, 2 * HOPS + 1]]
    names = owner_ref[...]
    offs = hops_ref[...]
    up = lax.broadcasted_iota(jnp.int32, (PAIRS, PAIRS), 0)
    along = lax.broadcasted_iota(jnp.int32, (PAIRS, PAIRS), 1)

    def upright(row):
        return jnp.sum(jnp.where(up == along, row, 0), axis=1, keepdims=True)

    def rank(column, row):
        return jnp.sum(
            jnp.where(jnp.logical_and(column == row, along < up), 1, 0), axis=1, keepdims=True
        )

    name, off = upright(names), upright(offs)
    target = name + rank(name, names) * NCHAN + 1
    place = off * 2 + rank(off, offs)
    spot = lax.broadcasted_iota(jnp.int32, (PAIRS, KEEP), 1)
    wanted = jnp.sum(jnp.where(place == spot, target, 0), axis=0, keepdims=True) - 1
    block = lax.broadcasted_iota(jnp.int32, (2 * NCHAN, KEEP), 0)
    chosen = jnp.where(wanted == block, 1.0, 0.0).astype(F32)
    pick = jnp.concatenate([chosen] * 3, axis=1).astype(BF16)
    cross_ref[pl.ds(32, KEEP - 32), :] = jnp.zeros((KEEP - 32, 2 * LANES), F32)

    def cross(h):
        for i in range(2):
            mine = rows_ref[mine_ref[0, 2 * h + i]].astype(F32)
            theirs = got_ref[h, i].astype(F32)
            mr, mi, tr, ti = mine[:16], mine[16:], theirs[:16], theirs[16:]
            at = pl.ds(2 * h + i, 1)
            cross_ref[at, pl.ds(0, LANES)] = jnp.sum(mr * tr + mi * ti, axis=0, keepdims=True)
            cross_ref[at, pl.ds(LANES, LANES)] = jnp.sum(mr * ti - mi * tr, axis=0, keepdims=True)

    cross(HOPS)
    for g in range(GROUPS):
        arrivals(got_ref, SHARE, hop_send, hop_recv.at[g]).wait_recv()
        for h in HOP_ORDER[g * SHARE : (g + 1) * SHARE]:
            cross(h)

    high, mid, low = split(cross_ref[...])
    mail = jnp.dot(pick, jnp.concatenate([high, mid, low], axis=0), preferred_element_type=F32)
    for s in range(2):
        for part in range(2):
            mail_ref[:, 2 * s + part, :] = mail[s * NCHAN : (s + 1) * NCHAN, part * LANES : (part + 1) * LANES]

    def own_copy(o, from_block):
        return pltpu.make_async_remote_copy(
            src_ref=mail_ref.at[o],
            dst_ref=out_ref.at[from_block],
            send_sem=own_send,
            recv_sem=own_recv,
            device_id=(o, mw),
            device_id_type=MESH,
        )

    for j in range(NCHAN):
        o = lax.rem(mc // 8 + 2 + j, 4) * 8 + j // 4

        @pl.when(o != mc)
        def _(o=o):
            own_copy(o, mc).start()

    keep_own = pltpu.make_async_copy(mail_ref.at[mc], out_ref.at[mc], own_local)
    keep_own.start()
    asks.wait_send()
    windows.wait_send()
    hops.wait_send()
    keep_own.wait()
    owns.wait_send()
    owns.wait_recv()


def local(traces, offsets, pair_source, pair_recv, pair_hop, pair_owner):
    pieces = traces.reshape(CH, REC // LANES, LANES).transpose(1, 0, 2)
    consts = [jnp.asarray(t) for t in tables()]
    anywhere = pl.BlockSpec(memory_space=pl.ANY)
    row = (1, PAIRS)
    out = pl.pallas_call(
        kernel,
        out_shape=pltpu.VMEM((NCHAN, 4, LANES), F32),
        in_specs=[anywhere] * 11,
        out_specs=anywhere,
        scratch_shapes=[
            pltpu.SMEM((1,), jnp.int32),
            pltpu.SMEM(row, jnp.int32),
            pltpu.SMEM(row, jnp.int32),
            pltpu.SMEM(row, jnp.int32),
            pltpu.VMEM(row, jnp.int32),
            pltpu.VMEM(row, jnp.int32),
            pltpu.VMEM((REC // LANES, CH, LANES), F32),
        ]
        + [pltpu.VMEM(c.shape, c.dtype) for c in consts]
        + [
            pltpu.VMEM((ROWS * CH, LANES), F32),
            pltpu.VMEM((2, BANDS + 2, CH, LANES), F32),
            pltpu.VMEM((BANDS, 16, LANES), BF16),
            pltpu.VMEM((NWIN, 16, LANES), BF16),
            pltpu.VMEM((CH, 32, LANES), BF16),
            pltpu.VMEM((OFFS, 2, 32, LANES), BF16),
            pltpu.VMEM((OFFS, 2, 32, LANES), BF16),
            pltpu.VMEM((KEEP, 2 * LANES), F32),
            pltpu.VMEM((NCHAN, 4, LANES), F32),
            pltpu.SMEM((1, LANES), jnp.int32),
            pltpu.SMEM((OFFS, LANES), jnp.int32),
            pltpu.SMEM((1, LANES), jnp.int32),
            pltpu.SemaphoreType.DMA((12,)),
        ]
        + [pltpu.SemaphoreType.DMA] * 5
        + [pltpu.SemaphoreType.DMA((GROUPS,))]
        + [pltpu.SemaphoreType.DMA] * 3,
        compiler_params=pltpu.CompilerParams(collective_id=0, has_side_effects=True),
        name="cross_spectra",
    )(offsets, pair_source, pair_recv, pair_hop, pair_owner.reshape(row), pieces, *consts)
    return out.reshape(2 * NCHAN, 2, LANES)


def solution(mesh):
    placed = (
        P("chan", "win"),
        P("win"),
        P("chan", None),
        P("chan", None),
        P("chan", None),
        P("chan", None),
    )
    return jax.shard_map(
        local, mesh=mesh, in_specs=placed, out_specs=P("chan", None, "win"), check_vma=False
    )
```
